32 devices in a mesh: ves: 16 (over z, y, x), sec: 2 (over core).
Axes of the slice: x: 2, y: 2, z: 4, core: 2. Of those that a mesh axis runs over, the one named last changes fastest.
Arguments:
- density: bfloat16 [8192, 3, 544], P(('ves', 'sec')), may hold values from -6 to 6
- analysis: bfloat16 [544, 289], replicated, may hold values from -0.25 to 0.25
- synthesis: bfloat16 [289, 544], replicated, may hold values from -0.375 to 0.375
- degree_gain: float32 [289], replicated, may hold values from 0.05 to 2
- near_kernel: bfloat16 [544, 544], replicated, may hold values from -0.25 to 0.25
- partners: int32 [8192, 4], P(('ves', 'sec')), may hold values from 0 to 8191, as said below
- pair_weight: float32 [8192, 4], P(('ves', 'sec')), may hold values from 0.2 to 1
- wall_list: int32 [512], P(('ves', 'sec')), may hold values from 0 to 8191, as said below
- coupling: bfloat16 [4096, 32], P(('ves', 'sec')), may hold values from -1 to 1
- wall_gain: float32 [4096], P(('ves', 'sec')), may hold values from 0.5 to 2
Outputs:
- velocity: float32 [8192, 3, 544], P(('ves', 'sec'))
The draws below stay inside these ranges and needn't reach their ends.
Inputs may be any that keep to these rules, and one draw needn't show every extreme that they name: `partners`: vesicles form blocks of 256 consecutive ids, block b in region b // 2, slot b % 2. A partner of vesicle i lies in the block of i, or among the last 64 vesicles of the block of the region below with the same slot, or among the first 64 of the block of the region above with the same slot. No vesicle is its own partner. `wall_list`: entry block b (entries b * 16 to b * 16 + 15) holds 16 distinct ids of vesicle block b.
All inputs are finite; a program needn't handle non-finite values.
Results may differ from the reference program's by a relative error of at most 0.0043.
Values may be sent and summed in bfloat16 or wider, within the bound.
A program may use at most 64 MiB of HBM per device.

```python
import math
import jax
import jax.numpy as jnp
from jax import lax

P_SIZE = 544
L = 289
K = 4
V_DEV = 256
NW_DEV = 16
Q_DEV = 128
H = 64
V = 8192
NWREG = 32
NQ = 4096
NWALL = 512
N_VES = 16
N_SEC = 2


def draw_partners(key, part):
    index = jnp.arange(V, dtype=jnp.int32)
    block = index // V_DEV
    local = (index % V_DEV)[:, None]
    region = (block // N_SEC)[:, None]
    slot = (block % N_SEC)[:, None]
    window = jax.random.randint(key, (V, K), 0, V_DEV + 2 * H, dtype=jnp.int32)
    window = jnp.where((region == 0) & (window < H), window + H, window)
    window = jnp.where((region == N_VES - 1) & (window >= V_DEV + H), window - H, window)
    window = jnp.where(window - H == local, H + (local + 1) % V_DEV, window)
    shift = jnp.where(window < H, -1, jnp.where(window >= V_DEV + H, 1, 0))
    inner = jnp.where(shift == -1, window + V_DEV - H, jnp.where(shift == 1, window - H - V_DEV, window - H))
    target = (region + shift) * N_SEC + slot
    return (target * V_DEV + inner).astype(jnp.int32)


def draw_wall_list(key, part):
    blocks = V // V_DEV
    keys = jax.random.split(key, blocks)
    chosen = jax.vmap(lambda one_key: jax.random.permutation(one_key, V_DEV)[:NW_DEV])(keys)
    chosen = chosen.astype(jnp.int32) + (jnp.arange(blocks, dtype=jnp.int32) * V_DEV)[:, None]
    return chosen.reshape(-1).astype(jnp.int32)


def shard_levels(stream_key, extent, pieces, low, top_value):
    loudness, own = 1.0, jax.random.fold_in(stream_key, 6)
    for axis_at, blocks in pieces:
        steps = jnp.exp(jax.random.uniform(jax.random.fold_in(own, axis_at), (blocks,), jnp.float32, low / len(pieces), top_value / len(pieces)))
        loudness = loudness * jnp.repeat(steps, extent[axis_at] // blocks).reshape([-1 if axis == axis_at else 1 for axis in range(len(extent))])
    return loudness


def normal_values(own_key, shape, deviation, limit, cuts=(), kind=jnp.bfloat16):
    loudness = shard_levels(own_key, shape, cuts, -0.22, 0.18) if cuts else 1.0
    entries = jax.random.normal(own_key, shape, jnp.float32) * deviation * loudness
    return jnp.minimum(jnp.maximum(entries, -limit), limit).astype(kind)


def setup_inputs(seed: int = 0) -> dict:
    seeds = jax.random.split(jax.random.key(seed), 11)
    density = normal_values(seeds[0], (V, 3, P_SIZE), 1.0, 6.0, ((0, 32),))
    analysis = normal_values(seeds[1], (P_SIZE, L), P_SIZE ** -0.5, 0.25)
    synthesis = normal_values(seeds[2], (L, P_SIZE), L ** -0.5, 0.375)
    degree_gain = jnp.clip(jnp.exp(jax.random.uniform(seeds[3], (L,), jnp.float32, math.log(0.05), math.log(2.0))), 0.05, 2.0)
    near_kernel = normal_values(seeds[4], (P_SIZE, P_SIZE), P_SIZE ** -0.5, 0.25)
    partners = draw_partners(jax.random.fold_in(seeds[10], 71), 0)
    pair_weight = jnp.clip(0.2 + 0.8 * jax.random.uniform(seeds[6], (V, K), jnp.float32) ** shard_levels(seeds[6], (V, K), ((0, 32),), -0.2, 0.2), 0.2, 1.0)
    wall_list = draw_wall_list(jax.random.fold_in(seeds[10], 71), 0)
    coupling = normal_values(seeds[8], (NQ, NWREG), NWREG ** -0.5, 1.0, ((0, 32),))
    wall_gain = jnp.clip(jnp.exp(math.log(2.0) - 1.3862944 * jax.random.uniform(seeds[9], (NQ,), jnp.float32) ** shard_levels(seeds[9], (NQ,), ((0, 32),), -0.2, 0.2)), 0.5, 2.0)
    return dict(density=density, analysis=analysis, synthesis=synthesis, degree_gain=degree_gain, near_kernel=near_kernel, partners=partners, pair_weight=pair_weight, wall_list=wall_list, coupling=coupling, wall_gain=wall_gain)


def reference(density, analysis, synthesis, degree_gain, near_kernel, partners, pair_weight, wall_list, coupling, wall_gain):
    blocks = V // V_DEV
    dens = density.reshape(blocks, V_DEV * 3, P_SIZE)

    def first(block_dens):
        coef = jnp.dot(block_dens, analysis, preferred_element_type=jnp.float32).astype(jnp.bfloat16)
        smooth = jnp.dot(coef, synthesis, preferred_element_type=jnp.float32).astype(jnp.bfloat16)
        return coef, smooth

    coef, smooth = lax.map(first, dens)
    smooth_flat = smooth.reshape(V, 3, P_SIZE)
    coef_flat = coef.reshape(V, 3 * L)
    region_ids = wall_list.reshape(N_VES, NWREG)
    region_g = coupling.reshape(N_VES, Q_DEV * N_SEC, NWREG)
    region_gain = wall_gain.reshape(N_VES, Q_DEV * N_SEC)

    def wall(args):
        ids, gmat, gain = args
        xmat = coef_flat[ids]
        wall_dens = (gain[:, None] * jnp.dot(gmat, xmat, preferred_element_type=jnp.float32)).astype(jnp.bfloat16)
        back = jnp.dot(gmat.T, wall_dens, preferred_element_type=jnp.float32)
        return back.astype(jnp.bfloat16)

    backs = lax.map(wall, (region_ids, region_g, region_gain))
    wall_coef = jnp.zeros((V, 3 * L), jnp.bfloat16).at[wall_list].set(backs.reshape(NWALL, 3 * L))

    def second(args):
        block_coef, ids, weights, wcoef = args
        scaled = (block_coef.astype(jnp.float32) * degree_gain).astype(jnp.bfloat16)
        self_vel = jnp.dot(scaled, synthesis, preferred_element_type=jnp.float32)
        gathered = smooth_flat[ids]
        mixed = jnp.zeros((V_DEV, 3, P_SIZE), jnp.float32)
        for k in range(K):
            mixed = mixed + weights[:, k, None, None] * gathered[:, k].astype(jnp.float32)
        mixed = mixed.astype(jnp.bfloat16).reshape(V_DEV * 3, P_SIZE)
        near_vel = jnp.dot(mixed, near_kernel, preferred_element_type=jnp.float32)
        wall_vel = jnp.dot(wcoef, synthesis, preferred_element_type=jnp.float32)
        return self_vel + near_vel + wall_vel

    out = lax.map(second, (coef, partners.reshape(blocks, V_DEV, K), pair_weight.reshape(blocks, V_DEV, K), wall_coef.reshape(blocks, V_DEV * 3, L)))
    return out.reshape(V, 3, P_SIZE)
```

```python
import functools

import jax
import jax.numpy as jnp
from jax import lax
from jax.experimental import pallas as pl
from jax.experimental.pallas import tpu as pltpu
from jax.sharding import PartitionSpec as P

MESH = pl.DeviceIdType.MESH
F32 = jnp.float32
BF16 = jnp.bfloat16


def dot(a, b, ca=1, cb=0):
    return lax.dot_general(a, b, (((ca,), (cb,)), ((), ())), preferred_element_type=F32)


def step_kernel(
    n_ves,
    n_sec,
    dens_ref,
    ana_ref,
    syn_ref,
    gain_ref,
    near_ref,
    part_ref,
    weight_ref,
    list_ref,
    coup_ref,
    wgain_ref,
    out_ref,
    coef_ref,
    mix_ref,
    tail01,
    tail2,
    head01,
    head2,
    recv01,
    recv2,
    halo2,
    pick_all,
    coup_all,
    gain_all,
    send_sem,
    recv_sem,
    wall_send,
    wall_recv,
):
    ves = lax.axis_index("ves")
    sec = lax.axis_index("sec")
    comps, num_points, count = dens_ref.shape
    num_coefs = ana_ref.shape[0]
    near_wall = list_ref.shape[0]
    edge = count // 4
    tile = 2 * edge
    cut = recv2.shape[1]
    top = num_coefs - cut
    has_left = ves > 0
    has_right = ves < n_ves - 1
    hops = range(1, n_sec)

    barrier = pltpu.get_barrier_semaphore()

    @pl.when(has_left)
    def _():
        pl.semaphore_signal(barrier, inc=1, device_id=(ves - 1, sec), device_id_type=MESH)

    @pl.when(has_right)
    def _():
        pl.semaphore_signal(barrier, inc=1, device_id=(ves + 1, sec), device_id_type=MESH)

    for hop in hops:
        peer = lax.rem(sec + hop, n_sec)
        pl.semaphore_signal(barrier, inc=1, device_id=(ves, peer), device_id_type=MESH)

    def halo_copy(src, dst, slot, piece, to):
        return pltpu.make_async_remote_copy(
            src_ref=src,
            dst_ref=dst.at[slot],
            send_sem=send_sem.at[slot, piece],
            recv_sem=recv_sem.at[slot, piece],
            device_id=(to, sec),
            device_id_type=MESH,
        )

    def up_copy(piece):
        src, dst = ((tail01, recv01), (tail2, recv2))[piece]
        return halo_copy(src, dst, 0, piece, ves + 1)

    def down_copy(piece):
        src, dst = ((head01, recv01), (head2, recv2))[piece]
        return halo_copy(src, dst, 1, piece, ves - 1)

    def wall_copy(hop, kind):
        src, dst = (
            (coup_ref, coup_all.at[hop - 1]),
            (wgain_ref, gain_all.at[hop - 1]),
            (pick_all.at[sec], pick_all.at[sec]),
        )[kind]
        return pltpu.make_async_remote_copy(
            src_ref=src,
            dst_ref=dst,
            send_sem=wall_send.at[kind, hop - 1],
            recv_sem=wall_recv.at[kind, hop - 1],
            device_id=(ves, lax.rem(sec + hop, n_sec)),
            device_id_type=MESH,
        )

    @pl.when(jnp.logical_not(has_left))
    def _():
        recv01[0] = jnp.zeros(recv01.shape[1:], BF16)
        recv2[0] = jnp.zeros(recv2.shape[1:], BF16)

    @pl.when(jnp.logical_not(has_right))
    def _():
        recv01[1] = jnp.zeros(recv01.shape[1:], BF16)
        recv2[1] = jnp.zeros(recv2.shape[1:], BF16)

    low = lax.broadcasted_iota(jnp.int32, (num_coefs, tile), 1) < edge
    ana = ana_ref[...]

    def analyse(c):
        full = dot(ana, dens_ref[c])
        coef_ref[c] = full.astype(BF16)
        return full[:, :tile], full[:, count - tile :]

    head_0, tail_0 = analyse(0)
    head_1, tail_1 = analyse(1)
    tail01[...] = jnp.where(low, pltpu.roll(tail_0, edge, 1), tail_1).astype(BF16)
    head01[...] = jnp.where(low, head_0, pltpu.roll(head_1, edge, 1)).astype(BF16)

    pl.semaphore_wait(barrier, n_sec - 1 + has_left.astype(jnp.int32) + has_right.astype(jnp.int32))

    @pl.when(has_right)
    def _():
        up_copy(0).start()

    @pl.when(has_left)
    def _():
        down_copy(0).start()

    for hop in hops:
        wall_copy(hop, 0).start()
        wall_copy(hop, 1).start()

    head_2, tail_2 = analyse(2)
    low2 = low[:cut]
    tail2[...] = jnp.where(low2, pltpu.roll(tail_2, edge, 1)[:cut], tail_2[top:]).astype(BF16)
    head2[...] = jnp.where(low2, head_2[:cut], pltpu.roll(head_2, edge, 1)[top:]).astype(BF16)

    @pl.when(has_right)
    def _():
        up_copy(1).start()

    @pl.when(has_left)
    def _():
        down_copy(1).start()

    base = (ves * n_sec + sec) * count

    def placing(rows, first):
        row = lax.broadcasted_iota(jnp.int32, (rows, count), 0)
        ids = jnp.full((rows, count), -1, jnp.int32)
        for j in range(near_wall):
            ids = jnp.where(row == first + j, list_ref[j] - base, ids)
        hit = ids == lax.broadcasted_iota(jnp.int32, (rows, count), 1)
        return jnp.where(hit, 1.0, 0.0).astype(BF16)

    choose = placing(near_wall, 0)
    for c in range(comps):
        pick_all[sec, c] = dot(choose, coef_ref[c], 1, 1).astype(BF16)
    for hop in hops:
        wall_copy(hop, 2).start()

    shift = part_ref[...] - base
    weight = weight_ref[...]

    def mixing(rows, start):
        want = lax.broadcasted_iota(jnp.int32, (rows, count), 0) + start
        total = jnp.zeros((rows, count), F32)
        for k in range(shift.shape[0]):
            total = total + jnp.where(shift[k : k + 1, :] == want, weight[k : k + 1, :], 0.0)
        high = total.astype(BF16)
        return high, (total - high.astype(F32)).astype(BF16)

    own_high, own_low = mixing(count, 0)
    left_high, left_low = mixing(edge, count - edge - n_sec * count)
    right_high, right_low = mixing(edge, n_sec * count)
    none = jnp.zeros((edge, count), BF16)
    first_high = jnp.concatenate([left_high, none, right_high, none], axis=0)
    first_low = jnp.concatenate([left_low, none, right_low, none], axis=0)
    second_high = jnp.concatenate([none, left_high, none, right_high], axis=0)
    second_low = jnp.concatenate([none, left_low, none, right_low], axis=0)

    square = (num_coefs, num_coefs)
    diagonal = lax.broadcasted_iota(jnp.int32, square, 0) == lax.broadcasted_iota(
        jnp.int32, square, 1
    )
    gain = jnp.sum(jnp.where(diagonal, gain_ref[...], 0.0), axis=1, keepdims=True)

    syn = syn_ref[...]
    for c in range(comps):
        smooth = dot(syn, coef_ref[c], 0, 0).astype(BF16)
        mix_ref[c] = dot(smooth, own_high) + dot(smooth, own_low)

    for hop in hops:
        for kind in range(3):
            wall_copy(hop, kind).wait()
    coup = jnp.concatenate([coup_ref[...]] + [coup_all[hop - 1] for hop in hops], axis=1)
    wgain = jnp.concatenate([wgain_ref[...]] + [gain_all[hop - 1] for hop in hops], axis=1)
    place = placing(near_wall * n_sec, sec * near_wall)
    for c in range(comps):
        picked = jnp.concatenate([pick_all[s, c] for s in range(n_sec)], axis=0)
        dens = (dot(picked, coup, 0, 0) * wgain).astype(BF16)
        back = dot(coup, dens, 1, 1).astype(BF16)
        wall = dot(back, place, 0, 0).astype(BF16)
        scaled = (coef_ref[c].astype(F32) * gain).astype(BF16)
        out_ref[c] = dot(syn, scaled, 0, 0) + dot(syn, wall, 0, 0)

    def receive(piece):
        @pl.when(has_left)
        def _():
            up_copy(piece).wait_recv()

        @pl.when(has_right)
        def _():
            down_copy(piece).wait_recv()

    def finish(c, halo, high, lower):
        mixed = (mix_ref[c] + dot(halo, high) + dot(halo, lower)).astype(BF16)
        out_ref[c] = out_ref[c] + dot(near_ref[...], mixed, 0, 0)

    receive(0)
    both = jnp.concatenate([recv01[0], recv01[1]], axis=1)
    halo = dot(syn, both, 0, 0).astype(BF16)
    finish(0, halo, first_high, first_low)
    finish(1, halo, second_high, second_low)

    receive(1)
    for side in range(2):
        lanes = slice(side * tile, (side + 1) * tile)
        flat = recv2[side].astype(F32)
        halo2[:top, lanes] = flat[:top].astype(BF16)
        halo2[top:, lanes] = pltpu.roll(flat, edge, 1).astype(BF16)
    halo = dot(syn, halo2[...], 0, 0).astype(BF16)
    finish(2, halo, first_high, first_low)

    for piece in range(2):

        @pl.when(has_right)
        def _():
            up_copy(piece).wait_send()

        @pl.when(has_left)
        def _():
            down_copy(piece).wait_send()


def shards(
    n_ves,
    n_sec,
    density,
    analysis,
    synthesis,
    degree_gain,
    near_kernel,
    partners,
    pair_weight,
    wall_list,
    coupling,
    wall_gain,
):
    count, comps, num_points = density.shape
    num_coefs = analysis.shape[1]
    near_wall = wall_list.shape[0]
    panels, region_wall = coupling.shape
    tile = count // 2
    top = num_coefs // 2 // 16 * 16
    cut = num_coefs - top
    others = max(n_sec - 1, 1)
    vmem = pl.BlockSpec(memory_space=pltpu.VMEM)
    specs = [vmem] * 10
    specs[7] = pl.BlockSpec(memory_space=pltpu.SMEM)
    out = pl.pallas_call(
        functools.partial(step_kernel, n_ves, n_sec),
        name="vesicle_step",
        out_shape=OUT((comps, num_points, count)),
        in_specs=specs,
        out_specs=vmem,
        scratch_shapes=[
            pltpu.VMEM((comps, num_coefs, count), BF16),
            pltpu.VMEM((comps, num_points, count), F32),
            pltpu.VMEM((num_coefs, tile), BF16),
            pltpu.VMEM((cut, tile), BF16),
            pltpu.VMEM((num_coefs, tile), BF16),
            pltpu.VMEM((cut, tile), BF16),
            pltpu.VMEM((2, num_coefs, tile), BF16),
            pltpu.VMEM((2, cut, tile), BF16),
            pltpu.VMEM((num_coefs, 2 * tile), BF16),
            pltpu.VMEM((n_sec, comps, near_wall, num_coefs), BF16),
            pltpu.VMEM((others, region_wall, panels), BF16),
            pltpu.VMEM((others, 1, panels), F32),
            pltpu.SemaphoreType.DMA((2, 2)),
            pltpu.SemaphoreType.DMA((2, 2)),
            pltpu.SemaphoreType.DMA((3, others)),
            pltpu.SemaphoreType.DMA((3, others)),
        ],
        compiler_params=pltpu.CompilerParams(
            collective_id=0, has_side_effects=True, vmem_limit_bytes=32 * 1024 * 1024
        ),
    )(
        density.transpose(1, 2, 0),
        analysis.T,
        synthesis,
        degree_gain.reshape(1, num_coefs),
        near_kernel,
        partners.T,
        pair_weight.T,
        wall_list,
        coupling.T,
        wall_gain.reshape(1, panels),
    )
    return out.transpose(2, 0, 1)


def OUT(shape):
    return jax.ShapeDtypeStruct(shape, F32)


def solution(mesh):
    n_ves, n_sec = mesh.shape["ves"], mesh.shape["sec"]
    return jax.shard_map(
        functools.partial(shards, n_ves, n_sec),
        mesh=mesh,
        in_specs=(
            P(("ves", "sec"), None, None),
            P(),
            P(),
            P(),
            P(),
            P(("ves", "sec"), None),
            P(("ves", "sec"), None),
            P(("ves", "sec")),
            P(("ves", "sec"), None),
            P(("ves", "sec")),
        ),
        out_specs=P(("ves", "sec"), None, None),
        check_vma=False,
    )
```

```python
import functools

import jax
import jax.numpy as jnp
from jax import lax
from jax.experimental import pallas as pl
from jax.experimental.pallas import tpu as pltpu
from jax.sharding import PartitionSpec as P

MESH = pl.DeviceIdType.MESH
F32 = jnp.float32
BF16 = jnp.bfloat16


def dot(a, b, ca=1, cb=0):
    return lax.dot_general(a, b, (((ca,), (cb,)), ((), ())), preferred_element_type=F32)


def step_kernel(
    n_ves,
    n_sec,
    dens_in,
    ana_in,
    syn_in,
    gain_ref,
    near_in,
    part_in,
    weight_in,
    list_in,
    coup_in,
    wgain_in,
    out_ref,
    dens_ref,
    ana_ref,
    syn_ref,
    near_ref,
    part_ref,
    weight_ref,
    list_ref,
    coup_ref,
    wgain_ref,
    syn_turned,
    near_turned,
    load_sem,
    coef_ref,
    mix_ref,
    tail01,
    tail2,
    head01,
    head2,
    recv01,
    recv2,
    halo2,
    pick_all,
    coup_all,
    gain_all,
    send_sem,
    recv_sem,
    wall_send,
    wall_recv,
):
    ves = lax.axis_index("ves")
    sec = lax.axis_index("sec")
    comps, _, count = dens_ref.shape
    num_coefs = ana_ref.shape[0]
    near_wall = list_ref.shape[0]
    edge = count // 4
    tile = 2 * edge
    cut = recv2.shape[1]
    top = num_coefs - cut
    has_left = ves > 0
    has_right = ves < n_ves - 1
    hops = range(1, n_sec)

    pairs = [(ana_in, ana_ref)]
    pairs += [(dens_in.at[c], dens_ref.at[c]) for c in range(comps)]
    pairs += [
        (list_in, list_ref),
        (part_in, part_ref),
        (weight_in, weight_ref),
        (syn_in, syn_ref),
        (coup_in, coup_ref),
        (wgain_in, wgain_ref),
        (near_in, near_ref),
    ]
    loads = [
        pltpu.make_async_copy(src, dst, load_sem.at[i]) for i, (src, dst) in enumerate(pairs)
    ]
    for load in loads:
        load.start()
    load_ana, *load_dens = loads[: comps + 1]
    load_list, load_part, load_weight, load_syn, load_coup, load_wgain, load_near = loads[comps + 1 :]

    barrier = pltpu.get_barrier_semaphore()

    @pl.when(has_left)
    def _():
        pl.semaphore_signal(barrier, inc=1, device_id=(ves - 1, sec), device_id_type=MESH)

    @pl.when(has_right)
    def _():
        pl.semaphore_signal(barrier, inc=1, device_id=(ves + 1, sec), device_id_type=MESH)

    for hop in hops:
        peer = lax.rem(sec + hop, n_sec)
        pl.semaphore_signal(barrier, inc=1, device_id=(ves, peer), device_id_type=MESH)

    def halo_copy(src, dst, slot, piece, to):
        return pltpu.make_async_remote_copy(
            src_ref=src,
            dst_ref=dst.at[slot],
            send_sem=send_sem.at[slot, piece],
            recv_sem=recv_sem.at[slot, piece],
            device_id=(to, sec),
            device_id_type=MESH,
        )

    def up_copy(piece):
        src, dst = ((tail01, recv01), (tail2, recv2))[piece]
        return halo_copy(src, dst, 0, piece, ves + 1)

    def down_copy(piece):
        src, dst = ((head01, recv01), (head2, recv2))[piece]
        return halo_copy(src, dst, 1, piece, ves - 1)

    def wall_copy(hop, kind):
        src, dst = (
            (coup_in, coup_all.at[hop - 1]),
            (wgain_in, gain_all.at[hop - 1]),
            (pick_all.at[sec], pick_all.at[sec]),
        )[kind]
        return pltpu.make_async_remote_copy(
            src_ref=src,
            dst_ref=dst,
            send_sem=wall_send.at[kind, hop - 1],
            recv_sem=wall_recv.at[kind, hop - 1],
            device_id=(ves, lax.rem(sec + hop, n_sec)),
            device_id_type=MESH,
        )

    @pl.when(jnp.logical_not(has_left))
    def _():
        recv01[0] = jnp.zeros(recv01.shape[1:], BF16)
        recv2[0] = jnp.zeros(recv2.shape[1:], BF16)

    @pl.when(jnp.logical_not(has_right))
    def _():
        recv01[1] = jnp.zeros(recv01.shape[1:], BF16)
        recv2[1] = jnp.zeros(recv2.shape[1:], BF16)

    low = lax.broadcasted_iota(jnp.int32, (num_coefs, tile), 1) < edge
    load_ana.wait()
    ana = ana_ref[...]

    def analyse(c):
        load_dens[c].wait()
        full = dot(ana, dens_ref[c])
        coef_ref[c] = full.astype(BF16)
        return full[:, :tile], full[:, count - tile :]

    head_0, tail_0 = analyse(0)
    head_1, tail_1 = analyse(1)
    tail01[...] = jnp.where(low, pltpu.roll(tail_0, edge, 1), tail_1).astype(BF16)
    head01[...] = jnp.where(low, head_0, pltpu.roll(head_1, edge, 1)).astype(BF16)

    pl.semaphore_wait(barrier, n_sec - 1 + has_left.astype(jnp.int32) + has_right.astype(jnp.int32))

    @pl.when(has_right)
    def _():
        up_copy(0).start()

    @pl.when(has_left)
    def _():
        down_copy(0).start()

    for hop in hops:
        wall_copy(hop, 0).start()
        wall_copy(hop, 1).start()

    head_2, tail_2 = analyse(2)
    low2 = low[:cut]
    tail2[...] = jnp.where(low2, pltpu.roll(tail_2, edge, 1)[:cut], tail_2[top:]).astype(BF16)
    head2[...] = jnp.where(low2, head_2[:cut], pltpu.roll(head_2, edge, 1)[top:]).astype(BF16)

    @pl.when(has_right)
    def _():
        up_copy(1).start()

    @pl.when(has_left)
    def _():
        down_copy(1).start()

    base = (ves * n_sec + sec) * count

    def placing(rows, first):
        row = lax.broadcasted_iota(jnp.int32, (rows, count), 0)
        ids = jnp.full((rows, count), -1, jnp.int32)
        for j in range(near_wall):
            ids = jnp.where(row == first + j, list_ref[j] - base, ids)
        hit = ids == lax.broadcasted_iota(jnp.int32, (rows, count), 1)
        return jnp.where(hit, 1.0, 0.0).astype(BF16)

    load_list.wait()
    choose = placing(near_wall, 0)
    for c in range(comps):
        pick_all[sec, c] = dot(choose, coef_ref[c], 1, 1).astype(BF16)
    for hop in hops:
        wall_copy(hop, 2).start()

    load_part.wait()
    load_weight.wait()
    shift = part_ref[...] - base
    weight = weight_ref[...]

    def mixing(rows, start):
        want = lax.broadcasted_iota(jnp.int32, (rows, count), 0) + start
        total = jnp.zeros((rows, count), F32)
        for k in range(shift.shape[0]):
            total = total + jnp.where(shift[k : k + 1, :] == want, weight[k : k + 1, :], 0.0)
        high = total.astype(BF16)
        return high, (total - high.astype(F32)).astype(BF16)

    own_high, own_low = mixing(count, 0)
    left_high, left_low = mixing(edge, count - edge - n_sec * count)
    right_high, right_low = mixing(edge, n_sec * count)
    none = jnp.zeros((edge, count), BF16)
    first_high = jnp.concatenate([left_high, none, right_high, none], axis=0)
    first_low = jnp.concatenate([left_low, none, right_low, none], axis=0)
    second_high = jnp.concatenate([none, left_high, none, right_high], axis=0)
    second_low = jnp.concatenate([none, left_low, none, right_low], axis=0)

    square = (num_coefs, num_coefs)
    diagonal = lax.broadcasted_iota(jnp.int32, square, 0) == lax.broadcasted_iota(
        jnp.int32, square, 1
    )
    gain = jnp.sum(jnp.where(diagonal, gain_ref[...].reshape(1, num_coefs), 0.0), axis=1, keepdims=True)

    load_syn.wait()
    syn_turned[...] = syn_ref[...].T
    load_near.wait()
    near_turned[...] = near_ref[...].T
    syn = syn_turned[...]
    for c in range(comps):
        smooth = dot(syn, coef_ref[c]).astype(BF16)
        mix_ref[c] = dot(smooth, own_high) + dot(smooth, own_low)

    for hop in hops:
        for kind in range(3):
            wall_copy(hop, kind).wait()
    load_coup.wait()
    load_wgain.wait()
    coup = jnp.concatenate([coup_ref[...]] + [coup_all[hop - 1] for hop in hops], axis=1)
    wgain = jnp.concatenate([wgain_ref[...]] + [gain_all[hop - 1] for hop in hops], axis=1)
    place = placing(near_wall * n_sec, sec * near_wall)
    for c in range(comps):
        picked = jnp.concatenate([pick_all[s, c] for s in range(n_sec)], axis=0)
        dens = (dot(picked, coup, 0, 0) * wgain).astype(BF16)
        back = dot(coup, dens, 1, 1).astype(BF16)
        wall = dot(back, place, 0, 0).astype(BF16)
        scaled = (coef_ref[c].astype(F32) * gain).astype(BF16)
        out_ref[c] = dot(syn, scaled) + dot(syn, wall)

    def receive(piece):
        @pl.when(has_left)
        def _():
            up_copy(piece).wait_recv()

        @pl.when(has_right)
        def _():
            down_copy(piece).wait_recv()

    def finish(c, halo, high, lower):
        mixed = (mix_ref[c] + dot(halo, high) + dot(halo, lower)).astype(BF16)
        out_ref[c] = out_ref[c] + dot(near_turned[...], mixed)

    receive(0)
    both = jnp.concatenate([recv01[0], recv01[1]], axis=1)
    halo = dot(syn, both).astype(BF16)
    finish(0, halo, first_high, first_low)
    finish(1, halo, second_high, second_low)

    receive(1)
    for side in range(2):
        lanes = slice(side * tile, (side + 1) * tile)
        flat = recv2[side].astype(F32)
        halo2[:top, lanes] = flat[:top].astype(BF16)
        halo2[top:, lanes] = pltpu.roll(flat, edge, 1).astype(BF16)
    halo = dot(syn, halo2[...]).astype(BF16)
    finish(2, halo, first_high, first_low)

    for piece in range(2):

        @pl.when(has_right)
        def _():
            up_copy(piece).wait_send()

        @pl.when(has_left)
        def _():
            down_copy(piece).wait_send()


def shards(
    n_ves,
    n_sec,
    density,
    analysis,
    synthesis,
    degree_gain,
    near_kernel,
    partners,
    pair_weight,
    wall_list,
    coupling,
    wall_gain,
):
    count, comps, num_points = density.shape
    num_coefs = analysis.shape[1]
    near_wall = wall_list.shape[0]
    panels, region_wall = coupling.shape
    tile = count // 2
    top = num_coefs // 2 // 16 * 16
    cut = num_coefs - top
    others = max(n_sec - 1, 1)
    vmem = pl.BlockSpec(memory_space=pltpu.VMEM)
    specs = [pl.BlockSpec(memory_space=pltpu.HBM)] * 10
    specs[3] = vmem
    out = pl.pallas_call(
        functools.partial(step_kernel, n_ves, n_sec),
        name="vesicle_step",
        out_shape=jax.ShapeDtypeStruct((comps, num_points, count), F32),
        in_specs=specs,
        out_specs=vmem,
        scratch_shapes=[
            pltpu.VMEM((comps, num_points, count), BF16),
            pltpu.VMEM((num_coefs, num_points), BF16),
            pltpu.VMEM((num_coefs, num_points), BF16),
            pltpu.VMEM((num_points, num_points), BF16),
            pltpu.VMEM(partners.shape[::-1], jnp.int32),
            pltpu.VMEM(partners.shape[::-1], F32),
            pltpu.SMEM((near_wall,), jnp.int32),
            pltpu.VMEM((region_wall, panels), BF16),
            pltpu.VMEM((1, panels), F32),
            pltpu.VMEM((num_points, num_coefs), BF16),
            pltpu.VMEM((num_points, num_points), BF16),
            pltpu.SemaphoreType.DMA((comps + 8,)),
            pltpu.VMEM((comps, num_coefs, count), BF16),
            pltpu.VMEM((comps, num_points, count), F32),
            pltpu.VMEM((num_coefs, tile), BF16),
            pltpu.VMEM((cut, tile), BF16),
            pltpu.VMEM((num_coefs, tile), BF16),
            pltpu.VMEM((cut, tile), BF16),
            pltpu.VMEM((2, num_coefs, tile), BF16),
            pltpu.VMEM((2, cut, tile), BF16),
            pltpu.VMEM((num_coefs, 2 * tile), BF16),
            pltpu.VMEM((n_sec, comps, near_wall, num_coefs), BF16),
            pltpu.VMEM((others, region_wall, panels), BF16),
            pltpu.VMEM((others, 1, panels), F32),
            pltpu.SemaphoreType.DMA((2, 2)),
            pltpu.SemaphoreType.DMA((2, 2)),
            pltpu.SemaphoreType.DMA((3, others)),
            pltpu.SemaphoreType.DMA((3, others)),
        ],
        compiler_params=pltpu.CompilerParams(
            collective_id=0, has_side_effects=True, vmem_limit_bytes=32 * 1024 * 1024
        ),
    )(
        *(
            pltpu.with_memory_space_constraint(array, pltpu.HBM)
            for array in (
                density.transpose(1, 2, 0),
                analysis.T,
                synthesis,
                degree_gain,
                near_kernel,
                partners.T,
                pair_weight.T,
                wall_list,
                coupling.T,
                wall_gain.reshape(1, panels),
            )
        )
    )
    return out.transpose(2, 0, 1)


def solution(mesh):
    n_ves, n_sec = mesh.shape["ves"], mesh.shape["sec"]
    return jax.shard_map(
        functools.partial(shards, n_ves, n_sec),
        mesh=mesh,
        in_specs=(
            P(("ves", "sec"), None, None),
            P(),
            P(),
            P(),
            P(),
            P(("ves", "sec"), None),
            P(("ves", "sec"), None),
            P(("ves", "sec")),
            P(("ves", "sec"), None),
            P(("ves", "sec")),
        ),
        out_specs=P(("ves", "sec"), None, None),
        check_vma=False,
    )
```

```python
import functools

import jax
import jax.numpy as jnp
from jax import lax
from jax.experimental import pallas as pl
from jax.experimental.pallas import tpu as pltpu
from jax.sharding import PartitionSpec as P

MESH = pl.DeviceIdType.MESH
F32 = jnp.float32
BF16 = jnp.bfloat16


def dot(a, b, ca=1, cb=0):
    return lax.dot_general(a, b, (((ca,), (cb,)), ((), ())), preferred_element_type=F32)


def step_kernel(
    n_ves,
    n_sec,
    dens_in,
    ana_in,
    syn_in,
    gain_ref,
    near_in,
    part_in,
    weight_in,
    list_in,
    coup_in,
    wgain_in,
    out_ref,
    dens_ref,
    ana_ref,
    syn_ref,
    near_ref,
    part_ref,
    weight_ref,
    list_ref,
    coup_ref,
    wgain_ref,
    syn_turned,
    both_high,
    both_low,
    load_sem,
    coef_ref,
    mix_ref,
    total_ref,
    tail_ref,
    head_ref,
    recv_ref,
    pick_all,
    coup_all,
    gain_all,
    send_sem,
    recv_sem,
    wall_send,
    wall_recv,
):
    ves = lax.axis_index("ves")
    sec = lax.axis_index("sec")
    comps, _, count = dens_ref.shape
    num_coefs = ana_ref.shape[0]
    near_wall = list_ref.shape[0]
    edge = count // 4
    tile = 2 * edge
    cut = recv_ref.shape[2]
    top = num_coefs - cut
    has_left = ves > 0
    has_right = ves < n_ves - 1
    hops = range(1, n_sec)

    pairs = [(ana_in, ana_ref)]
    pairs += [(dens_in.at[c], dens_ref.at[c]) for c in range(comps)]
    pairs += [
        (list_in, list_ref),
        (part_in, part_ref),
        (weight_in, weight_ref),
        (syn_in, syn_ref),
        (coup_in, coup_ref),
        (wgain_in, wgain_ref),
        (near_in, near_ref),
    ]
    loads = [
        pltpu.make_async_copy(src, dst, load_sem.at[i]) for i, (src, dst) in enumerate(pairs)
    ]
    for load in loads:
        load.start()
    load_ana, *load_dens = loads[: comps + 1]
    load_list, load_part, load_weight, load_syn, load_coup, load_wgain, load_near = loads[comps + 1 :]

    barrier = pltpu.get_barrier_semaphore()

    @pl.when(has_left)
    def _():
        pl.semaphore_signal(barrier, inc=1, device_id=(ves - 1, sec), device_id_type=MESH)

    @pl.when(has_right)
    def _():
        pl.semaphore_signal(barrier, inc=1, device_id=(ves + 1, sec), device_id_type=MESH)

    for hop in hops:
        peer = lax.rem(sec + hop, n_sec)
        pl.semaphore_signal(barrier, inc=1, device_id=(ves, peer), device_id_type=MESH)

    def halo_copy(src, side, c, to):
        return pltpu.make_async_remote_copy(
            src_ref=src.at[c],
            dst_ref=recv_ref.at[side, c],
            send_sem=send_sem.at[side, c],
            recv_sem=recv_sem.at[side, c],
            device_id=(to, sec),
            device_id_type=MESH,
        )

    def up_copy(c):
        return halo_copy(tail_ref, 0, c, ves + 1)

    def down_copy(c):
        return halo_copy(head_ref, 1, c, ves - 1)

    def wall_copy(hop, kind):
        src, dst = (
            (coup_in, coup_all.at[hop - 1]),
            (wgain_in, gain_all.at[hop - 1]),
            (pick_all.at[sec], pick_all.at[sec]),
        )[kind]
        return pltpu.make_async_remote_copy(
            src_ref=src,
            dst_ref=dst,
            send_sem=wall_send.at[kind, hop - 1],
            recv_sem=wall_recv.at[kind, hop - 1],
            device_id=(ves, lax.rem(sec + hop, n_sec)),
            device_id_type=MESH,
        )

    @pl.when(jnp.logical_not(has_left))
    def _():
        recv_ref[0] = jnp.zeros(recv_ref.shape[1:], BF16)

    @pl.when(jnp.logical_not(has_right))
    def _():
        recv_ref[1] = jnp.zeros(recv_ref.shape[1:], BF16)

    low = lax.broadcasted_iota(jnp.int32, (cut, tile), 1) < edge
    load_ana.wait()
    ana = ana_ref[...]

    for c in range(comps):
        load_dens[c].wait()
        full = dot(ana, dens_ref[c])
        coef_ref[c] = full.astype(BF16)
        head = full[:, :tile]
        tail = full[:, count - tile :]
        tail_ref[c] = jnp.where(low, pltpu.roll(tail, edge, 1)[:cut], tail[top:]).astype(BF16)
        head_ref[c] = jnp.where(low, head[:cut], pltpu.roll(head, edge, 1)[top:]).astype(BF16)
        if c == 0:
            sides = has_left.astype(jnp.int32) + has_right.astype(jnp.int32)
            pl.semaphore_wait(barrier, n_sec - 1 + sides)

        @pl.when(has_right)
        def _():
            up_copy(c).start()

        @pl.when(has_left)
        def _():
            down_copy(c).start()

    for hop in hops:
        wall_copy(hop, 0).start()
        wall_copy(hop, 1).start()

    base = (ves * n_sec + sec) * count

    def placing(rows, first):
        row = lax.broadcasted_iota(jnp.int32, (rows, count), 0)
        ids = jnp.full((rows, count), -1, jnp.int32)
        for j in range(near_wall):
            ids = jnp.where(row == first + j, list_ref[j] - base, ids)
        hit = ids == lax.broadcasted_iota(jnp.int32, (rows, count), 1)
        return jnp.where(hit, 1.0, 0.0).astype(BF16)

    load_list.wait()
    choose = placing(near_wall, 0)
    for c in range(comps):
        pick_all[sec, c] = dot(choose, coef_ref[c], 1, 1).astype(BF16)
    for hop in hops:
        wall_copy(hop, 2).start()

    load_part.wait()
    load_weight.wait()
    shift = part_ref[...] - base
    weight = weight_ref[...]

    def mixing(rows, start):
        want = lax.broadcasted_iota(jnp.int32, (rows, count), 0) + start
        total = jnp.zeros((rows, count), F32)
        for k in range(shift.shape[0]):
            total = total + jnp.where(shift[k : k + 1, :] == want, weight[k : k + 1, :], 0.0)
        high = total.astype(BF16)
        return high, (total - high.astype(F32)).astype(BF16)

    own_high, own_low = mixing(count, 0)
    left_high, left_low = mixing(edge, count - edge - n_sec * count)
    right_high, right_low = mixing(edge, n_sec * count)
    none = jnp.zeros((edge, count), BF16)
    first_high = jnp.concatenate([left_high, none, right_high, none], axis=0)
    first_low = jnp.concatenate([left_low, none, right_low, none], axis=0)
    second_high = jnp.concatenate([none, left_high, none, right_high], axis=0)
    second_low = jnp.concatenate([none, left_low, none, right_low], axis=0)

    square = (num_coefs, num_coefs)
    diagonal = lax.broadcasted_iota(jnp.int32, square, 0) == lax.broadcasted_iota(
        jnp.int32, square, 1
    )
    gain = jnp.sum(jnp.where(diagonal, gain_ref[...].reshape(1, num_coefs), 0.0), axis=1, keepdims=True)

    for c in range(comps):
        mix_ref[c] = dot(coef_ref[c], own_high) + dot(coef_ref[c], own_low)

    load_syn.wait()
    syn_turned[...] = syn_ref[...].T
    syn = syn_turned[...]
    load_near.wait()
    both = dot(near_ref[...].T, syn)
    both_high[...] = both.astype(BF16)
    both_low[...] = (both - both_high[...].astype(F32)).astype(BF16)

    for hop in hops:
        for kind in range(3):
            wall_copy(hop, kind).wait()
    load_coup.wait()
    load_wgain.wait()
    coup = jnp.concatenate([coup_ref[...]] + [coup_all[hop - 1] for hop in hops], axis=1)
    wgain = jnp.concatenate([wgain_ref[...]] + [gain_all[hop - 1] for hop in hops], axis=1)
    place = placing(near_wall * n_sec, sec * near_wall)
    for c in range(comps):
        picked = jnp.concatenate([pick_all[s, c] for s in range(n_sec)], axis=0)
        dens = (dot(picked, coup, 0, 0) * wgain).astype(BF16)
        back = dot(coup, dens, 1, 1).astype(BF16)
        wall = dot(back, place, 0, 0)
        scaled = (coef_ref[c].astype(F32) * gain).astype(BF16)
        out_ref[c] = dot(syn, scaled) + dot(syn, wall.astype(BF16))

    def receive(c):
        @pl.when(has_left)
        def _():
            up_copy(c).wait_recv()

        @pl.when(has_right)
        def _():
            down_copy(c).wait_recv()

    for c in range(comps):
        receive(c)
        halo = jnp.concatenate([recv_ref[0, c], recv_ref[1, c]], axis=1)
        first = dot(halo[:top], first_high) + dot(halo[:top], first_low)
        second = dot(halo, second_high) + dot(halo, second_low)
        total_ref[:top] = (mix_ref[c, :top] + first).astype(BF16)
        total_ref[top:] = (mix_ref[c, top:] + second).astype(BF16)
        total = total_ref[...]
        out_ref[c] = out_ref[c] + (dot(both_high[...], total) + dot(both_low[...], total))

    for c in range(comps):

        @pl.when(has_right)
        def _():
            up_copy(c).wait_send()

        @pl.when(has_left)
        def _():
            down_copy(c).wait_send()


def shards(
    n_ves,
    n_sec,
    density,
    analysis,
    synthesis,
    degree_gain,
    near_kernel,
    partners,
    pair_weight,
    wall_list,
    coupling,
    wall_gain,
):
    count, comps, num_points = density.shape
    num_coefs = analysis.shape[1]
    near_wall = wall_list.shape[0]
    panels, region_wall = coupling.shape
    tile = count // 2
    top = num_coefs // 2 // 16 * 16
    cut = num_coefs - top
    others = max(n_sec - 1, 1)
    vmem = pl.BlockSpec(memory_space=pltpu.VMEM)
    specs = [pl.BlockSpec(memory_space=pltpu.HBM)] * 10
    specs[3] = vmem
    out = pl.pallas_call(
        functools.partial(step_kernel, n_ves, n_sec),
        name="vesicle_step",
        out_shape=jax.ShapeDtypeStruct((comps, num_points, count), F32),
        in_specs=specs,
        out_specs=vmem,
        scratch_shapes=[
            pltpu.VMEM((comps, num_points, count), BF16),
            pltpu.VMEM((num_coefs, num_points), BF16),
            pltpu.VMEM((num_coefs, num_points), BF16),
            pltpu.VMEM((num_points, num_points), BF16),
            pltpu.VMEM(partners.shape[::-1], jnp.int32),
            pltpu.VMEM(partners.shape[::-1], F32),
            pltpu.SMEM((near_wall,), jnp.int32),
            pltpu.VMEM((region_wall, panels), BF16),
            pltpu.VMEM((1, panels), F32),
            pltpu.VMEM((num_points, num_coefs), BF16),
            pltpu.VMEM((num_points, num_coefs), BF16),
            pltpu.VMEM((num_points, num_coefs), BF16),
            pltpu.SemaphoreType.DMA((comps + 8,)),
            pltpu.VMEM((comps, num_coefs, count), BF16),
            pltpu.VMEM((comps, num_coefs, count), F32),
            pltpu.VMEM((num_coefs, count), BF16),
            pltpu.VMEM((comps, cut, tile), BF16),
            pltpu.VMEM((comps, cut, tile), BF16),
            pltpu.VMEM((2, comps, cut, tile), BF16),
            pltpu.VMEM((n_sec, comps, near_wall, num_coefs), BF16),
            pltpu.VMEM((others, region_wall, panels), BF16),
            pltpu.VMEM((others, 1, panels), F32),
            pltpu.SemaphoreType.DMA((2, comps)),
            pltpu.SemaphoreType.DMA((2, comps)),
            pltpu.SemaphoreType.DMA((3, others)),
            pltpu.SemaphoreType.DMA((3, others)),
        ],
        compiler_params=pltpu.CompilerParams(
            collective_id=0, has_side_effects=True, vmem_limit_bytes=32 * 1024 * 1024
        ),
    )(
        *(
            pltpu.with_memory_space_constraint(array, pltpu.HBM)
            for array in (
                density.transpose(1, 2, 0),
                analysis.T,
                synthesis,
                degree_gain,
                near_kernel,
                partners.T,
                pair_weight.T,
                wall_list,
                coupling.T,
                wall_gain.reshape(1, panels),
            )
        )
    )
    return out.transpose(2, 0, 1)


def solution(mesh):
    n_ves, n_sec = mesh.shape["ves"], mesh.shape["sec"]
    return jax.shard_map(
        functools.partial(shards, n_ves, n_sec),
        mesh=mesh,
        in_specs=(
            P(("ves", "sec"), None, None),
            P(),
            P(),
            P(),
            P(),
            P(("ves", "sec"), None),
            P(("ves", "sec"), None),
            P(("ves", "sec")),
            P(("ves", "sec"), None),
            P(("ves", "sec")),
        ),
        out_specs=P(("ves", "sec"), None, None),
        check_vma=False,
    )
```

```python
import functools

import jax
import jax.numpy as jnp
from jax import lax
from jax.experimental import pallas as pl
from jax.experimental.pallas import tpu as pltpu
from jax.sharding import PartitionSpec as P

MESH = pl.DeviceIdType.MESH
F32 = jnp.float32
BF16 = jnp.bfloat16


def dot(a, b, ca=1, cb=0):
    return lax.dot_general(a, b, (((ca,), (cb,)), ((), ())), preferred_element_type=F32)


def step_kernel(
    n_ves,
    n_sec,
    dens_in,
    ana_in,
    syn_in,
    gain_ref,
    near_in,
    part_in,
    weight_in,
    list_in,
    coup_in,
    wgain_in,
    out_ref,
    dens_ref,
    ana_ref,
    syn_ref,
    near_ref,
    part_ref,
    weight_ref,
    list_ref,
    coup_ref,
    wgain_ref,
    syn_turned,
    both_ref,
    load_sem,
    coef_ref,
    mix_ref,
    total_ref,
    tail_ref,
    head_ref,
    recv_ref,
    pick_all,
    coup_all,
    gain_all,
    send_sem,
    recv_sem,
    wall_send,
    wall_recv,
):
    ves = lax.axis_index("ves")
    sec = lax.axis_index("sec")
    comps, _, count = dens_ref.shape
    num_coefs = ana_ref.shape[0]
    near_wall = list_ref.shape[0]
    edge = count // 4
    tile = 2 * edge
    cut = recv_ref.shape[2]
    top = num_coefs - cut
    has_left = ves > 0
    has_right = ves < n_ves - 1
    hops = range(1, n_sec)

    barrier = pltpu.get_barrier_semaphore()

    @pl.when(has_left)
    def _():
        pl.semaphore_signal(barrier, inc=1, device_id=(ves - 1, sec), device_id_type=MESH)

    @pl.when(has_right)
    def _():
        pl.semaphore_signal(barrier, inc=1, device_id=(ves + 1, sec), device_id_type=MESH)

    for hop in hops:
        peer = lax.rem(sec + hop, n_sec)
        pl.semaphore_signal(barrier, inc=1, device_id=(ves, peer), device_id_type=MESH)

    pairs = [(ana_in, ana_ref)]
    pairs += [(dens_in.at[c], dens_ref.at[c]) for c in range(comps)]
    pairs += [
        (list_in, list_ref),
        (part_in, part_ref),
        (weight_in, weight_ref),
        (syn_in, syn_ref),
        (coup_in, coup_ref),
        (wgain_in, wgain_ref),
        (near_in, near_ref),
    ]
    loads = [
        pltpu.make_async_copy(src, dst, load_sem.at[i]) for i, (src, dst) in enumerate(pairs)
    ]
    for load in loads:
        load.start()
    load_ana, *load_dens = loads[: comps + 1]
    load_list, load_part, load_weight, load_syn, load_coup, load_wgain, load_near = loads[comps + 1 :]

    def halo_copy(src, side, c, to):
        return pltpu.make_async_remote_copy(
            src_ref=src.at[c],
            dst_ref=recv_ref.at[side, c],
            send_sem=send_sem.at[side, c],
            recv_sem=recv_sem.at[side, c],
            device_id=(to, sec),
            device_id_type=MESH,
        )

    def up_copy(c):
        return halo_copy(tail_ref, 0, c, ves + 1)

    def down_copy(c):
        return halo_copy(head_ref, 1, c, ves - 1)

    def wall_copy(hop, kind):
        src, dst = (
            (coup_in, coup_all.at[hop - 1]),
            (wgain_in, gain_all.at[hop - 1]),
            (pick_all.at[sec], pick_all.at[sec]),
        )[kind]
        return pltpu.make_async_remote_copy(
            src_ref=src,
            dst_ref=dst,
            send_sem=wall_send.at[kind, hop - 1],
            recv_sem=wall_recv.at[kind, hop - 1],
            device_id=(ves, lax.rem(sec + hop, n_sec)),
            device_id_type=MESH,
        )

    @pl.when(jnp.logical_not(has_left))
    def _():
        recv_ref[0] = jnp.zeros(recv_ref.shape[1:], BF16)

    @pl.when(jnp.logical_not(has_right))
    def _():
        recv_ref[1] = jnp.zeros(recv_ref.shape[1:], BF16)

    low = lax.broadcasted_iota(jnp.int32, (cut, tile), 1) < edge
    load_ana.wait()
    ana = ana_ref[...]

    for c in range(comps):
        load_dens[c].wait()
        full = dot(ana, dens_ref[c])
        coef_ref[c] = full.astype(BF16)
        head = full[:, :tile]
        tail = full[:, count - tile :]
        tail_ref[c] = jnp.where(low, pltpu.roll(tail, edge, 1)[:cut], tail[top:]).astype(BF16)
        head_ref[c] = jnp.where(low, head[:cut], pltpu.roll(head, edge, 1)[top:]).astype(BF16)
        if c == 0:
            sides = has_left.astype(jnp.int32) + has_right.astype(jnp.int32)
            pl.semaphore_wait(barrier, n_sec - 1 + sides)

        @pl.when(has_right)
        def _():
            up_copy(c).start()

        @pl.when(has_left)
        def _():
            down_copy(c).start()

    for hop in hops:
        wall_copy(hop, 0).start()
        wall_copy(hop, 1).start()

    base = (ves * n_sec + sec) * count

    def placing(rows, first):
        row = lax.broadcasted_iota(jnp.int32, (rows, count), 0)
        ids = jnp.full((rows, count), -1, jnp.int32)
        for j in range(near_wall):
            ids = jnp.where(row == first + j, list_ref[j] - base, ids)
        hit = ids == lax.broadcasted_iota(jnp.int32, (rows, count), 1)
        return jnp.where(hit, 1.0, 0.0).astype(BF16)

    load_list.wait()
    choose = placing(near_wall, 0)
    for c in range(comps):
        pick_all[sec, c] = dot(choose, coef_ref[c], 1, 1).astype(BF16)
    for hop in hops:
        wall_copy(hop, 2).start()

    load_part.wait()
    load_weight.wait()
    shift = part_ref[...] - base
    weight = weight_ref[...]

    def mixing(rows, start):
        want = lax.broadcasted_iota(jnp.int32, (rows, count), 0) + start
        total = jnp.zeros((rows, count), F32)
        for k in range(shift.shape[0]):
            total = total + jnp.where(shift[k : k + 1, :] == want, weight[k : k + 1, :], 0.0)
        return total.astype(BF16)

    own_mix = mixing(count, 0)
    left_mix = mixing(edge, count - edge - n_sec * count)
    right_mix = mixing(edge, n_sec * count)
    none = jnp.zeros((edge, count), BF16)
    first_mix = jnp.concatenate([left_mix, none, right_mix, none], axis=0)
    second_mix = jnp.concatenate([none, left_mix, none, right_mix], axis=0)

    square = (num_coefs, num_coefs)
    diagonal = lax.broadcasted_iota(jnp.int32, square, 0) == lax.broadcasted_iota(
        jnp.int32, square, 1
    )
    gain = jnp.sum(jnp.where(diagonal, gain_ref[...].reshape(1, num_coefs), 0.0), axis=1, keepdims=True)

    for c in range(comps):
        mix_ref[c] = dot(coef_ref[c], own_mix)

    load_syn.wait()
    syn_turned[...] = syn_ref[...].T
    syn = syn_turned[...]
    load_near.wait()
    both_ref[...] = dot(near_ref[...].T, syn).astype(BF16)

    for hop in hops:
        for kind in range(3):
            wall_copy(hop, kind).wait()
    load_coup.wait()
    load_wgain.wait()
    coup = jnp.concatenate([coup_ref[...]] + [coup_all[hop - 1] for hop in hops], axis=1)
    wgain = jnp.concatenate([wgain_ref[...]] + [gain_all[hop - 1] for hop in hops], axis=1)
    place = placing(near_wall * n_sec, sec * near_wall)
    for c in range(comps):
        picked = jnp.concatenate([pick_all[s, c] for s in range(n_sec)], axis=0)
        dens = (dot(picked, coup, 0, 0) * wgain).astype(BF16)
        back = dot(coup, dens, 1, 1).astype(BF16)
        wall = dot(back, place, 0, 0)
        scaled = coef_ref[c].astype(F32) * gain
        out_ref[c] = dot(syn, (scaled + wall).astype(BF16))

    def receive(c):
        @pl.when(has_left)
        def _():
            up_copy(c).wait_recv()

        @pl.when(has_right)
        def _():
            down_copy(c).wait_recv()

    for c in range(comps):
        receive(c)
        halo = jnp.concatenate([recv_ref[0, c], recv_ref[1, c]], axis=1)
        first = dot(halo[:top], first_mix)
        second = dot(halo, second_mix)
        total_ref[:top] = (mix_ref[c, :top] + first).astype(BF16)
        total_ref[top:] = (mix_ref[c, top:] + second).astype(BF16)
        total = total_ref[...]
        out_ref[c] = out_ref[c] + dot(both_ref[...], total)

    for c in range(comps):

        @pl.when(has_right)
        def _():
            up_copy(c).wait_send()

        @pl.when(has_left)
        def _():
            down_copy(c).wait_send()


def shards(
    n_ves,
    n_sec,
    density,
    analysis,
    synthesis,
    degree_gain,
    near_kernel,
    partners,
    pair_weight,
    wall_list,
    coupling,
    wall_gain,
):
    count, comps, num_points = density.shape
    num_coefs = analysis.shape[1]
    near_wall = wall_list.shape[0]
    panels, region_wall = coupling.shape
    tile = count // 2
    top = num_coefs // 2 // 16 * 16
    cut = num_coefs - top
    others = max(n_sec - 1, 1)
    vmem = pl.BlockSpec(memory_space=pltpu.VMEM)
    specs = [pl.BlockSpec(memory_space=pltpu.HBM)] * 10
    specs[3] = vmem
    out = pl.pallas_call(
        functools.partial(step_kernel, n_ves, n_sec),
        name="vesicle_step",
        out_shape=jax.ShapeDtypeStruct((comps, num_points, count), F32),
        in_specs=specs,
        out_specs=vmem,
        scratch_shapes=[
            pltpu.VMEM((comps, num_points, count), BF16),
            pltpu.VMEM((num_coefs, num_points), BF16),
            pltpu.VMEM((num_coefs, num_points), BF16),
            pltpu.VMEM((num_points, num_points), BF16),
            pltpu.VMEM(partners.shape[::-1], jnp.int32),
            pltpu.VMEM(partners.shape[::-1], F32),
            pltpu.SMEM((near_wall,), jnp.int32),
            pltpu.VMEM((region_wall, panels), BF16),
            pltpu.VMEM((1, panels), F32),
            pltpu.VMEM((num_points, num_coefs), BF16),
            pltpu.VMEM((num_points, num_coefs), BF16),
            pltpu.SemaphoreType.DMA((comps + 8,)),
            pltpu.VMEM((comps, num_coefs, count), BF16),
            pltpu.VMEM((comps, num_coefs, count), F32),
            pltpu.VMEM((num_coefs, count), BF16),
            pltpu.VMEM((comps, cut, tile), BF16),
            pltpu.VMEM((comps, cut, tile), BF16),
            pltpu.VMEM((2, comps, cut, tile), BF16),
            pltpu.VMEM((n_sec, comps, near_wall, num_coefs), BF16),
            pltpu.VMEM((others, region_wall, panels), BF16),
            pltpu.VMEM((others, 1, panels), F32),
            pltpu.SemaphoreType.DMA((2, comps)),
            pltpu.SemaphoreType.DMA((2, comps)),
            pltpu.SemaphoreType.DMA((3, others)),
            pltpu.SemaphoreType.DMA((3, others)),
        ],
        compiler_params=pltpu.CompilerParams(
            collective_id=0, has_side_effects=True, vmem_limit_bytes=32 * 1024 * 1024
        ),
    )(
        *(
            pltpu.with_memory_space_constraint(array, pltpu.HBM)
            for array in (
                density.transpose(1, 2, 0),
                analysis.T,
                synthesis,
                degree_gain,
                near_kernel,
                partners.T,
                pair_weight.T,
                wall_list,
                coupling.T,
                wall_gain.reshape(1, panels),
            )
        )
    )
    return out.transpose(2, 0, 1)


def solution(mesh):
    n_ves, n_sec = mesh.shape["ves"], mesh.shape["sec"]
    return jax.shard_map(
        functools.partial(shards, n_ves, n_sec),
        mesh=mesh,
        in_specs=(
            P(("ves", "sec"), None, None),
            P(),
            P(),
            P(),
            P(),
            P(("ves", "sec"), None),
            P(("ves", "sec"), None),
            P(("ves", "sec")),
            P(("ves", "sec"), None),
            P(("ves", "sec")),
        ),
        out_specs=P(("ves", "sec"), None, None),
        check_vma=False,
    )
```

```python
import functools

import jax
import jax.numpy as jnp
from jax import lax
from jax.experimental import pallas as pl
from jax.experimental.pallas import tpu as pltpu
from jax.sharding import PartitionSpec as P

MESH = pl.DeviceIdType.MESH
F32 = jnp.float32
BF16 = jnp.bfloat16


def dot(a, b, ca=1, cb=0):
    return lax.dot_general(a, b, (((ca,), (cb,)), ((), ())), preferred_element_type=F32)


def step_kernel(
    n_ves,
    n_sec,
    dens_in,
    ana_in,
    syn_in,
    gain_ref,
    near_in,
    part_in,
    weight_in,
    list_in,
    coup_in,
    wgain_in,
    out_ref,
    dens_ref,
    ana_ref,
    syn_ref,
    near_ref,
    part_ref,
    weight_ref,
    list_ref,
    coup_ref,
    wgain_ref,
    syn_turned,
    both_ref,
    load_sem,
    coef_ref,
    mix_ref,
    total_ref,
    tail_ref,
    head_ref,
    recv_ref,
    pick_all,
    coup_all,
    gain_all,
    send_sem,
    recv_sem,
    wall_send,
    wall_recv,
):
    ves = lax.axis_index("ves")
    sec = lax.axis_index("sec")
    comps, _, count = dens_ref.shape
    num_coefs = ana_ref.shape[0]
    near_wall = list_ref.shape[0]
    edge = count // 4
    tile = 2 * edge
    cut = recv_ref.shape[2]
    top = num_coefs - cut
    has_left = ves > 0
    has_right = ves < n_ves - 1
    hops = range(1, n_sec)

    barrier = pltpu.get_barrier_semaphore()

    @pl.when(has_left)
    def _():
        pl.semaphore_signal(barrier, inc=1, device_id=(ves - 1, sec), device_id_type=MESH)

    @pl.when(has_right)
    def _():
        pl.semaphore_signal(barrier, inc=1, device_id=(ves + 1, sec), device_id_type=MESH)

    for hop in hops:
        peer = lax.rem(sec + hop, n_sec)
        pl.semaphore_signal(barrier, inc=1, device_id=(ves, peer), device_id_type=MESH)

    pairs = [(ana_in, ana_ref)]
    pairs += [(dens_in.at[c], dens_ref.at[c]) for c in range(comps)]
    pairs += [
        (list_in, list_ref),
        (part_in, part_ref),
        (weight_in, weight_ref),
        (coup_in, coup_ref),
        (wgain_in, wgain_ref),
        (syn_in, syn_ref),
        (near_in, near_ref),
    ]
    loads = [
        pltpu.make_async_copy(src, dst, load_sem.at[i]) for i, (src, dst) in enumerate(pairs)
    ]
    for load in loads[:-2]:
        load.start()
    load_ana, *load_dens = loads[: comps + 1]
    load_list, load_part, load_weight, load_coup, load_wgain, load_syn, load_near = loads[comps + 1 :]

    def halo_copy(src, side, c, to):
        return pltpu.make_async_remote_copy(
            src_ref=src.at[c],
            dst_ref=recv_ref.at[side, c],
            send_sem=send_sem.at[side, c],
            recv_sem=recv_sem.at[side, c],
            device_id=(to, sec),
            device_id_type=MESH,
        )

    def up_copy(c):
        return halo_copy(tail_ref, 0, c, ves + 1)

    def down_copy(c):
        return halo_copy(head_ref, 1, c, ves - 1)

    def wall_copy(hop, kind):
        src, dst = (
            (coup_in, coup_all.at[hop - 1]),
            (wgain_in, gain_all.at[hop - 1]),
            (pick_all.at[sec], pick_all.at[sec]),
        )[kind]
        return pltpu.make_async_remote_copy(
            src_ref=src,
            dst_ref=dst,
            send_sem=wall_send.at[kind, hop - 1],
            recv_sem=wall_recv.at[kind, hop - 1],
            device_id=(ves, lax.rem(sec + hop, n_sec)),
            device_id_type=MESH,
        )

    @pl.when(jnp.logical_not(has_left))
    def _():
        recv_ref[0] = jnp.zeros(recv_ref.shape[1:], BF16)

    @pl.when(jnp.logical_not(has_right))
    def _():
        recv_ref[1] = jnp.zeros(recv_ref.shape[1:], BF16)

    low = lax.broadcasted_iota(jnp.int32, (cut, tile), 1) < edge
    load_ana.wait()
    ana = ana_ref[...]

    for c in range(comps):
        load_dens[c].wait()
        full = dot(ana, dens_ref[c])
        coef_ref[c] = full.astype(BF16)
        head = full[:, :tile]
        tail = full[:, count - tile :]
        tail_ref[c] = jnp.where(low, pltpu.roll(tail, edge, 1)[:cut], tail[top:]).astype(BF16)
        head_ref[c] = jnp.where(low, head[:cut], pltpu.roll(head, edge, 1)[top:]).astype(BF16)
        if c == 0:
            sides = has_left.astype(jnp.int32) + has_right.astype(jnp.int32)
            pl.semaphore_wait(barrier, n_sec - 1 + sides)

        @pl.when(has_right)
        def _():
            up_copy(c).start()

        @pl.when(has_left)
        def _():
            down_copy(c).start()

        if c == 0:
            load_syn.start()
            load_near.start()

    for hop in hops:
        wall_copy(hop, 0).start()
        wall_copy(hop, 1).start()

    base = (ves * n_sec + sec) * count

    def placing(rows, first):
        row = lax.broadcasted_iota(jnp.int32, (rows, count), 0)
        ids = jnp.full((rows, count), -1, jnp.int32)
        for j in range(near_wall):
            ids = jnp.where(row == first + j, list_ref[j] - base, ids)
        hit = ids == lax.broadcasted_iota(jnp.int32, (rows, count), 1)
        return jnp.where(hit, 1.0, 0.0).astype(BF16)

    load_list.wait()
    choose = placing(near_wall, 0)
    for c in range(comps):
        pick_all[sec, c] = dot(choose, coef_ref[c], 1, 1).astype(BF16)
    for hop in hops:
        wall_copy(hop, 2).start()

    load_part.wait()
    load_weight.wait()
    shift = part_ref[...] - base
    weight = weight_ref[...]

    def mixing(rows, start):
        want = lax.broadcasted_iota(jnp.int32, (rows, count), 0) + start
        total = jnp.zeros((rows, count), F32)
        for k in range(shift.shape[0]):
            total = total + jnp.where(shift[k : k + 1, :] == want, weight[k : k + 1, :], 0.0)
        return total.astype(BF16)

    own_mix = mixing(count, 0)
    left_mix = mixing(edge, count - edge - n_sec * count)
    right_mix = mixing(edge, n_sec * count)
    none = jnp.zeros((edge, count), BF16)
    first_mix = jnp.concatenate([left_mix, none, right_mix, none], axis=0)
    second_mix = jnp.concatenate([none, left_mix, none, right_mix], axis=0)

    square = (num_coefs, num_coefs)
    diagonal = lax.broadcasted_iota(jnp.int32, square, 0) == lax.broadcasted_iota(
        jnp.int32, square, 1
    )
    gain = jnp.sum(jnp.where(diagonal, gain_ref[...].reshape(1, num_coefs), 0.0), axis=1, keepdims=True)

    for c in range(comps):
        mix_ref[c] = dot(coef_ref[c], own_mix)

    load_syn.wait()
    syn_turned[...] = syn_ref[...].T
    syn = syn_turned[...]
    load_near.wait()
    both_ref[...] = dot(near_ref[...].T, syn).astype(BF16)

    for hop in hops:
        for kind in range(3):
            wall_copy(hop, kind).wait()
    load_coup.wait()
    load_wgain.wait()
    coup = jnp.concatenate([coup_ref[...]] + [coup_all[hop - 1] for hop in hops], axis=1)
    wgain = jnp.concatenate([wgain_ref[...]] + [gain_all[hop - 1] for hop in hops], axis=1)
    place = placing(near_wall * n_sec, sec * near_wall)
    for c in range(comps):
        picked = jnp.concatenate([pick_all[s, c] for s in range(n_sec)], axis=0)
        dens = (dot(picked, coup, 0, 0) * wgain).astype(BF16)
        back = dot(coup, dens, 1, 1).astype(BF16)
        wall = dot(back, place, 0, 0)
        scaled = coef_ref[c].astype(F32) * gain
        out_ref[c] = dot(syn, (scaled + wall).astype(BF16))

    def receive(c):
        @pl.when(has_left)
        def _():
            up_copy(c).wait_recv()

        @pl.when(has_right)
        def _():
            down_copy(c).wait_recv()

    for c in range(comps):
        receive(c)
        halo = jnp.concatenate([recv_ref[0, c], recv_ref[1, c]], axis=1)
        first = dot(halo[:top], first_mix)
        second = dot(halo, second_mix)
        total_ref[:top] = (mix_ref[c, :top] + first).astype(BF16)
        total_ref[top:] = (mix_ref[c, top:] + second).astype(BF16)
        total = total_ref[...]
        out_ref[c] = out_ref[c] + dot(both_ref[...], total)

    for c in range(comps):

        @pl.when(has_right)
        def _():
            up_copy(c).wait_send()

        @pl.when(has_left)
        def _():
            down_copy(c).wait_send()


def shards(
    n_ves,
    n_sec,
    density,
    analysis,
    synthesis,
    degree_gain,
    near_kernel,
    partners,
    pair_weight,
    wall_list,
    coupling,
    wall_gain,
):
    count, comps, num_points = density.shape
    num_coefs = analysis.shape[1]
    near_wall = wall_list.shape[0]
    panels, region_wall = coupling.shape
    tile = count // 2
    top = num_coefs // 2 // 16 * 16
    cut = num_coefs - top
    others = max(n_sec - 1, 1)
    vmem = pl.BlockSpec(memory_space=pltpu.VMEM)
    specs = [pl.BlockSpec(memory_space=pltpu.HBM)] * 10
    specs[3] = vmem
    out = pl.pallas_call(
        functools.partial(step_kernel, n_ves, n_sec),
        name="vesicle_step",
        out_shape=jax.ShapeDtypeStruct((comps, num_points, count), F32),
        in_specs=specs,
        out_specs=vmem,
        scratch_shapes=[
            pltpu.VMEM((comps, num_points, count), BF16),
            pltpu.VMEM((num_coefs, num_points), BF16),
            pltpu.VMEM((num_coefs, num_points), BF16),
            pltpu.VMEM((num_points, num_points), BF16),
            pltpu.VMEM(partners.shape[::-1], jnp.int32),
            pltpu.VMEM(partners.shape[::-1], F32),
            pltpu.SMEM((near_wall,), jnp.int32),
            pltpu.VMEM((region_wall, panels), BF16),
            pltpu.VMEM((1, panels), F32),
            pltpu.VMEM((num_points, num_coefs), BF16),
            pltpu.VMEM((num_points, num_coefs), BF16),
            pltpu.SemaphoreType.DMA((comps + 8,)),
            pltpu.VMEM((comps, num_coefs, count), BF16),
            pltpu.VMEM((comps, num_coefs, count), F32),
            pltpu.VMEM((num_coefs, count), BF16),
            pltpu.VMEM((comps, cut, tile), BF16),
            pltpu.VMEM((comps, cut, tile), BF16),
            pltpu.VMEM((2, comps, cut, tile), BF16),
            pltpu.VMEM((n_sec, comps, near_wall, num_coefs), BF16),
            pltpu.VMEM((others, region_wall, panels), BF16),
            pltpu.VMEM((others, 1, panels), F32),
            pltpu.SemaphoreType.DMA((2, comps)),
            pltpu.SemaphoreType.DMA((2, comps)),
            pltpu.SemaphoreType.DMA((3, others)),
            pltpu.SemaphoreType.DMA((3, others)),
        ],
        compiler_params=pltpu.CompilerParams(
            collective_id=0, has_side_effects=True, vmem_limit_bytes=32 * 1024 * 1024
        ),
    )(
        *(
            pltpu.with_memory_space_constraint(array, pltpu.HBM)
            for array in (
                density.transpose(1, 2, 0),
                analysis.T,
                synthesis,
                degree_gain,
                near_kernel,
                partners.T,
                pair_weight.T,
                wall_list,
                coupling.T,
                wall_gain.reshape(1, panels),
            )
        )
    )
    return out.transpose(2, 0, 1)


def solution(mesh):
    n_ves, n_sec = mesh.shape["ves"], mesh.shape["sec"]
    return jax.shard_map(
        functools.partial(shards, n_ves, n_sec),
        mesh=mesh,
        in_specs=(
            P(("ves", "sec"), None, None),
            P(),
            P(),
            P(),
            P(),
            P(("ves", "sec"), None),
            P(("ves", "sec"), None),
            P(("ves", "sec")),
            P(("ves", "sec"), None),
            P(("ves", "sec")),
        ),
        out_specs=P(("ves", "sec"), None, None),
        check_vma=False,
    )
```
